32 devices in a mesh: loop: 8 (over y, x, core), orb: 4 (over z).
Axes of the slice: x: 2, y: 2, z: 4, core: 2. Of those that a mesh axis runs over, the one named last changes fastest.
Arguments:
- cholesky: bfloat16 [4096, 65536], P('loop', 'orb'), may hold values from -0.0234375 to 0.0234375
- green_half: bfloat16 [384, 65536], P('loop', 'orb'), may hold values from -6 to 6
- partners: int32 [64, 2], replicated, may hold values from 0 to 383, as said below
Outputs:
- green_copied: bfloat16 [384, 65536], P('loop', 'orb')
- force_bias: float32 [384, 4096], P('orb', 'loop')
The draws below stay inside these ranges and needn't reach their ends.
Inputs may be any that keep to these rules, and one draw needn't show every extreme that they name: `partners`: column 0 is a source walker, column 1 a destination walker. Destinations are distinct, sources are distinct, and no source is a destination. Each block of 48 consecutive walkers holds exactly 8 destinations and exactly 8 sources.
All inputs are finite; a program needn't handle non-finite values.
Results may differ from the reference program's by a relative error of at most 0.001.
Values may be sent and summed in bfloat16 or wider, within the bound.
No kernel may reach another device: no remote copies, remote signals or barrier semaphores. Data moves between devices by JAX's collectives and lax.ppermute only.
A program may use at most 64 MiB of HBM per device.

```python
import jax
import jax.numpy as jnp
from jax import lax

NCHOL = 4096
WALK_DEV = 48
EV_DEV = 8
PAIRS = 65536
WALKERS = 384


def draw_partners(key, part):
    blocks = WALKERS // WALK_DEV
    block_keys = jax.random.split(jax.random.fold_in(key, 11), blocks)
    orders = jax.vmap(lambda block_key: jax.random.permutation(block_key, WALK_DEV))(block_keys).astype(jnp.int32)
    base = (jnp.arange(blocks, dtype=jnp.int32) * WALK_DEV)[:, None]
    targets = (orders[:, :EV_DEV] + base).reshape(-1)
    sources = (orders[:, EV_DEV:2 * EV_DEV] + base).reshape(-1)
    pairing = jax.random.permutation(jax.random.fold_in(key, 12), blocks * EV_DEV)
    listed = jnp.stack([sources[pairing], targets], axis=1)
    shuffle = jax.random.permutation(jax.random.fold_in(key, 13), blocks * EV_DEV)
    return listed[shuffle].astype(jnp.int32)


def with_spikes(drawn, own_key, source, target, shards_of, factor):
    def block_of(position):
        return (jnp.arange(drawn.shape[position]) // (drawn.shape[position] // shards_of)).reshape((-1,) + (1,) * (drawn.ndim - 1 - position))

    one_side = jax.random.permutation(own_key, shards_of)[block_of(target)]
    second = (block_of(target) + shards_of // 2) % shards_of
    return jnp.where((block_of(source) == one_side) | (block_of(source) == second), factor * drawn, drawn)


def steps_of(rng, extent, shards, least, top_value):
    factor_of = 1.0
    for position, shards_of in shards:
        steps = jax.random.uniform(jax.random.fold_in(jax.random.fold_in(rng, 6), position), (shards_of,), jnp.float32, least / len(shards), top_value / len(shards))
        factor_of = factor_of * jnp.repeat(jnp.exp(steps), extent[position] // shards_of).reshape((-1,) + (1,) * (len(extent) - 1 - position))
    return factor_of


def noise(own_key, extent, width, reach, cuts=(), kind=jnp.bfloat16):
    entries = jax.random.normal(own_key, extent, jnp.float32) * width
    if len(cuts) > 0:
        entries = steps_of(own_key, extent, cuts, -0.22, 0.18) * entries
    return jnp.clip(entries, min=-reach, max=reach).astype(kind)


def bell_draw_with(rng, extent, scale, most, shards, heavy, kind=jnp.bfloat16):
    result = scale * jax.random.normal(rng, extent, jnp.float32)
    if shards:
        result = result * steps_of(rng, extent, shards, -0.22, 0.18)
    return jnp.clip(with_spikes(result, jax.random.fold_in(rng, 3), *heavy), -most, most).astype(kind)


def setup_inputs(seed: int = 0) -> dict:
    streams_of = jax.random.split(jax.random.key(seed), 4)
    cholesky = noise(streams_of[0], (NCHOL, PAIRS), PAIRS ** -0.5, 0.0234375, ((0, 8), (1, 4)))
    green_half = bell_draw_with(streams_of[1], (WALKERS, PAIRS), 1.0, 6.0, ((0, 8), (1, 4)), (1, 0, 8, 2.0))
    partners = draw_partners(jax.random.fold_in(streams_of[3], 71), 0)
    return dict(cholesky=cholesky, green_half=green_half, partners=partners)


def reference(cholesky, green_half, partners):
    green_copied = green_half.at[partners[:, 1]].set(green_half[partners[:, 0]])

    def block_bias(walker_rows):
        return lax.dot_general(walker_rows, cholesky, (((1,), (1,)), ((), ())), preferred_element_type=jnp.float32)

    stacked = lax.map(block_bias, green_copied.reshape(WALKERS // WALK_DEV, WALK_DEV, PAIRS))
    return green_copied, stacked.reshape(WALKERS, NCHOL)
```

```python
import functools

import jax
import jax.numpy as jnp
from jax import lax
from jax.experimental import pallas as pl
from jax.experimental.pallas import tpu as pltpu
from jax.sharding import PartitionSpec as P


VMEM = pl.BlockSpec(memory_space=pltpu.VMEM)
SMEM = pl.BlockSpec(memory_space=pltpu.SMEM)
ANY = pl.BlockSpec(memory_space=pl.ANY)
I32 = jnp.int32
F32 = jnp.float32
BF16 = jnp.bfloat16
CONTRACT_LAST = (((1,), (1,)), ((), ()))


def iota(shape, axis):
    return lax.broadcasted_iota(I32, shape, axis)


def one_hot(condition):
    return jnp.where(condition, 1.0, 0.0).astype(BF16)


def dot(a, b):
    return jnp.dot(a, b, preferred_element_type=F32)


def exact_pick(select, values):
    high = values.astype(BF16)
    rest = values - high.astype(F32)
    middle = rest.astype(BF16)
    low = (rest - middle.astype(F32)).astype(BF16)
    return dot(select, high) + dot(select, middle) + dot(select, low)


def params(megabytes=None, **kw):
    if megabytes is not None:
        kw["vmem_limit_bytes"] = megabytes << 20
    return pltpu.CompilerParams(**kw)


def slot_of(offset, odd):
    swapped = jnp.where((offset == 2) | (offset == 3), offset + 2, jnp.where((offset == 4) | (offset == 5), offset - 2, offset))
    return jnp.where(odd == 1, swapped, offset)


def live_position(walker, first, sources, targets, per_block, axis):
    count = lambda condition: jnp.sum(condition.astype(I32), axis=axis, keepdims=True)
    is_source = count(sources == walker) > 0
    is_target = count(targets == walker) > 0
    sources_before = count((sources >= first) & (sources < walker))
    targets_before = count((targets >= first) & (targets < walker))
    plain = per_block + walker - first - sources_before - targets_before
    return jnp.where(is_target, -1, jnp.where(is_source, sources_before, plain)), is_target


def select_kernel(per_block, spans, tile, place, partners, green, *refs):
    outs, (held, sem) = refs[: len(spans)], refs[len(spans) :]
    rows, width = green.shape
    tiles = width // tile
    copies = [
        pltpu.make_async_copy(green.at[:, pl.ds(t * tile, tile)], held.at[:, pl.ds(t * tile, tile)], sem.at[t])
        for t in range(tiles)
    ]
    for copy in copies:
        copy.start()
    first = place[0] * rows
    events = partners[...]
    shape = (events.shape[0], rows)
    walker = iota((1, rows), 1) + first
    position, _ = live_position(walker, first, events[:, 0:1], events[:, 1:2], per_block, 0)
    live = rows - per_block
    select = one_hot(iota((live, rows), 0) == position)
    for t in range(tiles):
        copies[t].wait()
        picked = dot(select, held[:, t * tile : (t + 1) * tile]).astype(BF16)
        for out, (low, high, left, right) in zip(outs, spans):
            if left <= t * tile < right:
                out[:, t * tile - left : (t + 1) * tile - left] = picked[low:high]


def select_rows(place, partners, green, per_block, spans, tile):
    rows, width = green.shape
    return pl.pallas_call(
        functools.partial(select_kernel, per_block, spans, tile),
        in_specs=[SMEM, VMEM, ANY],
        out_specs=[VMEM] * len(spans),
        out_shape=[jax.ShapeDtypeStruct((h - l, b - a), BF16) for l, h, a, b in spans],
        scratch_shapes=[pltpu.VMEM((rows, width), BF16), pltpu.SemaphoreType.DMA((width // tile,))],
        compiler_params=params(8),
        cost_estimate=pl.CostEstimate(flops=2 * rows * rows * width, bytes_accessed=4 * rows * width, transcendentals=0),
        name="select_rows",
    )(place, partners, green)


def table_kernel(rows, blocks, orbs, per_block, phases, place, partners, *outs):
    mine, orb = place[0], place[1]
    odd = lax.bitwise_and(mine, 1)
    group = blocks // orbs
    events = partners[...]
    count = events.shape[0]
    source, target = events[:, 0:1], events[:, 1:2]
    eye = iota((count, count), 0) == iota((count, count), 1)
    turn = lambda column: jnp.sum(jnp.where(eye, column, 0), axis=0, keepdims=True)
    block_of = lambda walker: sum((walker >= rows * i).astype(I32) for i in range(1, blocks))
    source_row, target_row = turn(source), turn(target)
    source_block, target_block = block_of(source), block_of(target)
    source_block_row, target_block_row = turn(source_block), turn(target_block)
    rank = lambda own, own_block, other, other_block: jnp.sum(
        ((own_block == other_block) & (other < own)).astype(I32), axis=1, keepdims=True
    )
    source_rank = rank(source, source_block, source_row, source_block_row)
    target_rank_row = turn(rank(target, target_block, target_row, target_block_row))
    source_slot = slot_of(lax.bitwise_xor(source_block, mine), odd)
    target_orb_row = sum((target_block_row >= group * i).astype(I32) for i in range(1, orbs))
    outs = list(outs)
    first_rows = phases[0][1]
    for number, (low, high) in enumerate(phases):
        size = high - low
        extra = group * per_block if number == 0 else 0
        send = outs.pop(0)
        for j in range(orbs):
            to = lax.bitwise_xor(orb, j)
            t = iota((group * size + extra, 1), 0)
            inside = sum((t >= size * i).astype(I32) for i in range(1, group))
            column = slot_of(lax.bitwise_xor(to * group + inside, mine), odd) * size + t - inside * size
            column = jnp.where(t < group * size, column, -1)
            table = jnp.where(column == iota((1, blocks * size), 1), 1.0, 0.0)
            if extra:
                out_row = group * size + (target_block_row - target_orb_row * group) * per_block + target_rank_row
                row_hot = one_hot((t == out_row) & (target_orb_row == to))
                column_hot = one_hot(source_slot * size + source_rank == iota((1, blocks * size), 1))
                table = table + dot(row_hot, column_hot)
            send[j] = table.astype(BF16)
    total = group * rows
    w = iota((total, 1), 0)
    inside = sum((w >= rows * i).astype(I32) for i in range(1, group))
    walker = w + orb * total
    first = orb * total + inside * rows
    position, is_target = live_position(walker, first, source_row, target_row, per_block, 1)
    target_before = jnp.sum(((target_row >= first) & (target_row < walker)).astype(I32), axis=1, keepdims=True)
    for number, (low, high) in enumerate(phases):
        size = high - low
        extra = group * per_block if number == 0 else 0
        column = jnp.where((position >= low) & (position < high), inside * size + position - low, -1)
        if extra:
            column = jnp.where(is_target, group * size + inside * per_block + target_before, column)
        outs.pop(0)[...] = one_hot(column == iota((1, group * size + extra), 1))
    local = iota((rows, 1), 0) + mine * rows
    event_hot = one_hot(local == target_row)
    source_hot = one_hot(source_slot * per_block + source_rank == iota((1, blocks * per_block), 1))
    outs.pop(0)[...] = dot(event_hot, source_hot).astype(BF16)


def make_tables(place, partners, rows, blocks, orbs, per_block, phases):
    group = blocks // orbs
    shapes = []
    extra = [group * per_block] + [0] * (len(phases) - 1)
    for (low, high), more in zip(phases, extra):
        shapes.append((orbs, group * (high - low) + more, blocks * (high - low)))
    for (low, high), more in zip(phases, extra):
        shapes.append((group * rows, group * (high - low) + more))
    shapes.append((rows, blocks * per_block))
    outs = pl.pallas_call(
        functools.partial(table_kernel, rows, blocks, orbs, per_block, phases),
        in_specs=[SMEM, VMEM],
        out_specs=[VMEM] * len(shapes),
        out_shape=[jax.ShapeDtypeStruct(s, BF16) for s in shapes],
        compiler_params=params(8),
        cost_estimate=pl.CostEstimate(flops=10_000_000, bytes_accessed=1_000_000, transcendentals=0),
        name="make_tables",
    )(place, partners)
    n = len(phases)
    return outs[:n], outs[n : 2 * n], outs[2 * n]


def contract_kernel(slots, offset, tile, has_total, has_table, *refs):
    refs = list(refs)
    pieces = [refs.pop(0) for _ in range(slots)]
    cholesky = refs.pop(0)
    total = refs.pop(0) if has_total else None
    table = refs.pop(0) if has_table else None
    size, width = pieces[0].shape
    if has_table:
        outs, acc = refs[:-1], refs[-1]
    else:
        acc = refs[0]
    acc[...] = total[...] if has_total else jnp.zeros_like(acc)

    @pl.loop(0, width // tile)
    def _(k):
        here = pl.ds(pl.multiple_of(k * tile, tile), tile)
        there = pl.ds(pl.multiple_of(offset + k * tile, tile), tile)
        held = jnp.concatenate([piece[:, here] for piece in pieces], axis=0)
        acc[...] += lax.dot_general(held, cholesky[:, there], CONTRACT_LAST, preferred_element_type=F32)

    if has_table:
        for j, out in enumerate(outs):
            out[...] = exact_pick(table[j], acc[...])


def contract(pieces, cholesky, offset, total, table, tile):
    size, width = pieces[0].shape
    rows, vectors = len(pieces) * size, cholesky.shape[0]
    operands = list(pieces) + [cholesky]
    if total is not None:
        operands.append(total)
    if table is not None:
        operands.append(table)
        out_shape = [jax.ShapeDtypeStruct((table.shape[1], vectors), F32)] * table.shape[0]
        scratch = [pltpu.VMEM((rows, vectors), F32)]
    else:
        out_shape = [jax.ShapeDtypeStruct((rows, vectors), F32)]
        scratch = []
    outs = pl.pallas_call(
        functools.partial(contract_kernel, len(pieces), offset, tile, total is not None, table is not None),
        in_specs=[VMEM] * len(operands),
        out_specs=[VMEM] * len(out_shape),
        out_shape=out_shape,
        scratch_shapes=scratch,
        compiler_params=params(12),
        cost_estimate=pl.CostEstimate(
            flops=2 * max(rows, 256) * vectors * width, bytes_accessed=2 * vectors * width, transcendentals=0
        ),
        name="contract",
    )(*operands)
    return outs


def copy_kernel(slots, per_block, pick, green, *refs):
    pieces, out = refs[:slots], refs[slots]
    table = pick[...]
    sources = jnp.concatenate([piece[0:per_block, :] for piece in pieces], axis=0)
    copied = dot(table, sources).astype(BF16)
    hit = jnp.max(table.astype(F32), axis=1, keepdims=True) > 0
    out[...] = jnp.where(hit, copied, green[...])


def copy_rows(pick, green, pieces, per_block, tile):
    rows, width = green.shape
    size = pieces[0].shape[0]
    columns = lambda k: (0, k)
    return pl.pallas_call(
        functools.partial(copy_kernel, len(pieces), per_block),
        grid=(width // tile,),
        in_specs=[VMEM, pl.BlockSpec((rows, tile), columns)] + [pl.BlockSpec((size, tile), columns)] * len(pieces),
        out_specs=pl.BlockSpec((rows, tile), columns),
        out_shape=jax.ShapeDtypeStruct((rows, width), BF16),
        compiler_params=params(12),
        cost_estimate=pl.CostEstimate(flops=2 * rows * 64 * width, bytes_accessed=8 * rows * width, transcendentals=0),
        name="copy_rows",
    )(pick, green, *pieces)


def finish_kernel(orbs, groups, has_base, *refs):
    refs = list(refs)
    out = refs.pop()
    result = refs.pop(0)[...] if has_base else None
    for _ in range(groups):
        order = refs.pop(0)[...]
        parts = [refs.pop(0)[...] for _ in range(orbs)]
        term = exact_pick(order, functools.reduce(jnp.add, parts))
        result = term if result is None else result + term
    out[...] = result


def finish(base, groups):
    orbs = len(groups[0][1])
    operands = [] if base is None else [base]
    for order, parts in groups:
        operands += [order, *parts]
    rows, vectors = groups[0][0].shape[0], groups[0][1][0].shape[1]
    return pl.pallas_call(
        functools.partial(finish_kernel, orbs, len(groups), base is not None),
        in_specs=[VMEM] * len(operands),
        out_specs=VMEM,
        out_shape=jax.ShapeDtypeStruct((rows, vectors), F32),
        compiler_params=params(8),
        cost_estimate=pl.CostEstimate(flops=10_000_000, bytes_accessed=1_000_000, transcendentals=0),
        name="finish",
    )(*operands)


def gather_pieces(own, count):
    send = lambda x, step: lax.ppermute(x, "loop", [(i, i ^ step(i)) for i in range(count)])
    sibling = lambda x: send(x, lambda i: 1)
    ahead = lambda x: send(x, lambda i: 4 if i & 1 else 2)
    aside = lambda x: send(x, lambda i: 2 if i & 1 else 4)
    s0 = sibling(own)
    m1 = ahead(own)
    m2 = ahead(s0)
    f = aside(m1)
    s1 = sibling(m1)
    s2 = sibling(m2)
    s3 = sibling(f)
    return [own, s0, m1, m2, s2, s1, f, s3]


PHASES = ((16, 1), (16, 1), (8, 2))


def local_phased(cholesky, green_half, partners):
    blocks, orbs = lax.axis_size("loop"), lax.axis_size("orb")
    rows, width = green_half.shape
    per_block = partners.shape[0] // blocks
    tile = 1024
    place = jnp.stack([lax.axis_index("loop"), lax.axis_index("orb")]).astype(I32)
    spans, phases, low = [], [], 0
    for size, cuts in PHASES:
        for c in range(cuts):
            spans.append((low, low + size, c * width // cuts, (c + 1) * width // cuts))
        phases.append((low, low + size))
        low += size
    own = list(select_rows(place, partners, green_half, per_block, spans, 2048))
    sends, orders, pick = make_tables(place, partners, rows, blocks, orbs, per_block, tuple(phases))
    new_green, groups = None, []
    pieces_of = [gather_pieces(piece, blocks) for piece in own]
    for number, (size, cuts) in enumerate(PHASES):
        total = None
        for c in range(cuts):
            pieces = pieces_of.pop(0)
            last = c == cuts - 1
            outs = contract(pieces, cholesky, c * width // cuts, total, sends[number] if last else None, tile)
            total = None if last else outs[0]
            if number == 0:
                new_green = copy_rows(pick, green_half, pieces, per_block, 4096)
        parts = [outs[0]]
        for j in range(orbs - 1, 0, -1):
            parts.append(lax.ppermute(outs[j], "orb", [(i, i ^ j) for i in range(orbs)]))
        groups.append((orders[number], parts))
    base = finish(None, groups[:-1])
    return new_green, finish(base, groups[-1:])


def contract_plain(shard_rows, cholesky):
    return lax.dot_general(shard_rows, cholesky, CONTRACT_LAST, preferred_element_type=F32)


def local_gathered(cholesky, green_half, partners):
    loop_count = lax.axis_size("loop")
    block_rows = green_half.shape[0]
    walkers = block_rows * loop_count
    per_block = partners.shape[0] // loop_count
    sources, targets = partners[:, 0], partners[:, 1]
    first_row = lax.axis_index("loop") * block_rows
    walker_index = jnp.arange(walkers, dtype=I32)
    hits = targets[None, :] == walker_index[:, None]
    overwritten = jnp.any(hits, axis=1)
    anchor = jnp.where(overwritten, jnp.sum(jnp.where(hits, sources[None, :], 0), axis=1), walker_index)
    local_flags = lax.dynamic_slice_in_dim(overwritten, first_row, block_rows)
    local_targets = jnp.nonzero(local_flags, size=per_block)[0].astype(I32)
    local_anchor = jnp.take(anchor, first_row + local_targets)
    shard_rows = lax.all_gather(green_half, "loop", axis=0, tiled=True)
    bias = contract_plain(shard_rows, cholesky)
    select = (local_anchor[:, None] == walker_index[None, :]).astype(BF16)
    copied = dot(select, shard_rows).astype(BF16)
    new_green = green_half.at[local_targets].set(copied)
    full_bias = jnp.take(bias, anchor, axis=0)
    return new_green, lax.psum_scatter(full_bias, "orb", scatter_dimension=0, tiled=True)


def solution(mesh):
    blocks, orbs = mesh.shape["loop"], mesh.shape["orb"]
    cube = blocks == 2**3 and orbs & (orbs - 1) == 0 and blocks % orbs == 0
    return jax.shard_map(
        local_phased if cube else local_gathered,
        mesh=mesh,
        in_specs=(P("loop", "orb"), P("loop", "orb"), P()),
        out_specs=(P("loop", "orb"), P("orb", "loop")),
        check_vma=False,
    )
```

```python
import functools

import jax
import jax.numpy as jnp
from jax import lax
from jax.experimental import pallas as pl
from jax.experimental.pallas import tpu as pltpu
from jax.sharding import PartitionSpec as P


VMEM = pl.BlockSpec(memory_space=pltpu.VMEM)
HBM = pl.BlockSpec(memory_space=pltpu.HBM)
I32 = jnp.int32
F32 = jnp.float32
BF16 = jnp.bfloat16
CONTRACT_LAST = (((1,), (1,)), ((), ()))


def iota(shape, axis):
    return lax.broadcasted_iota(I32, shape, axis)


def one_hot(condition):
    return jnp.where(condition, 1.0, 0.0).astype(BF16)


def turn(line, axis):
    count = max(line.shape)
    eye = iota((count, count), 0) == iota((count, count), 1)
    return jnp.sum(jnp.where(eye, line, 0), axis=axis, keepdims=True)


def dot(a, b):
    return jnp.dot(a, b, preferred_element_type=F32)


def exact_pick(select, values, turned=False):
    high = values.astype(BF16)
    rest = values - high.astype(F32)
    middle = rest.astype(BF16)
    low = (rest - middle.astype(F32)).astype(BF16)
    numbers = CONTRACT_LAST if turned else (((1,), (0,)), ((), ()))
    take = lambda piece: lax.dot_general(select, piece, numbers, preferred_element_type=F32)
    return take(high) + take(middle) + take(low)


def hbm(x):
    return pltpu.with_memory_space_constraint(x, pltpu.HBM)


def params(megabytes=None, **kw):
    if megabytes is not None:
        kw["vmem_limit_bytes"] = megabytes << 20
    return pltpu.CompilerParams(**kw)


def slot_of(offset, odd):
    swapped = jnp.where((offset == 2) | (offset == 3), offset + 2, jnp.where((offset == 4) | (offset == 5), offset - 2, offset))
    return jnp.where(odd == 1, swapped, offset)


def live_position(walker, first, sources, targets, per_block, axis):
    count = lambda condition: jnp.sum(condition.astype(I32), axis=axis, keepdims=True)
    is_source = count(sources == walker) > 0
    is_target = count(targets == walker) > 0
    sources_before = count((sources >= first) & (sources < walker))
    targets_before = count((targets >= first) & (targets < walker))
    plain = per_block + walker - first - sources_before - targets_before
    return jnp.where(is_target, -1, jnp.where(is_source, sources_before, plain)), is_target


def select_kernel(per_block, spans, begin, tile, events, green, *refs):
    outs, (partners, held, event_sem, sem) = refs[: len(spans)], refs[len(spans) :]
    fetch = pltpu.make_async_copy(events, partners, event_sem)
    fetch.start()
    rows, width = held.shape
    tiles = width // tile
    copies = [
        pltpu.make_async_copy(
            green.at[:, pl.ds(begin + t * tile, tile)], held.at[:, pl.ds(t * tile, tile)], sem.at[t]
        )
        for t in range(tiles)
    ]
    for copy in copies:
        copy.start()
    first = lax.axis_index("loop") * rows
    fetch.wait()
    source, target = turn(partners[0:1, :], 1), turn(partners[1:2, :], 1)
    walker = iota((1, rows), 1) + first
    position, _ = live_position(walker, first, source, target, per_block, 0)
    live = rows - per_block
    select = one_hot(iota((live, rows), 0) == position)
    for t in range(tiles):
        copies[t].wait()
        picked = dot(select, held[:, t * tile : (t + 1) * tile]).astype(BF16)
        for out, (low, high, left, right) in zip(outs, spans):
            at = begin + t * tile
            if left <= at < right:
                out[:, at - left : at - left + tile] = picked[low:high]


def select_rows(partners, green, per_block, spans, tile):
    rows, begin = green.shape[0], min(span[2] for span in spans)
    width = max(span[3] for span in spans) - begin
    return pl.pallas_call(
        functools.partial(select_kernel, per_block, spans, begin, tile),
        in_specs=[HBM, HBM],
        out_specs=[VMEM] * len(spans),
        out_shape=[jax.ShapeDtypeStruct((h - l, b - a), BF16) for l, h, a, b in spans],
        scratch_shapes=[
            pltpu.VMEM(partners.shape, I32),
            pltpu.VMEM((rows, width), BF16),
            pltpu.SemaphoreType.DMA,
            pltpu.SemaphoreType.DMA((width // tile,)),
        ],
        compiler_params=params(8),
        cost_estimate=pl.CostEstimate(flops=2 * rows * rows * width, bytes_accessed=4 * rows * width, transcendentals=0),
        name="select_rows",
    )(hbm(partners), hbm(green))


def table_kernel(rows, blocks, orbs, per_block, phases, partners, *outs):
    mine, orb = lax.axis_index("loop"), lax.axis_index("orb")
    odd = lax.bitwise_and(mine, 1)
    group = blocks // orbs
    source_row, target_row = partners[0:1, :], partners[1:2, :]
    source, target = turn(source_row, 1), turn(target_row, 1)
    block_of = lambda walker: sum((walker >= rows * i).astype(I32) for i in range(1, blocks))
    source_block, target_block = block_of(source), block_of(target)
    source_block_row, target_block_row = block_of(source_row), block_of(target_row)
    rank = lambda own, own_block, other, other_block: jnp.sum(
        ((own_block == other_block) & (other < own)).astype(I32), axis=1, keepdims=True
    )
    source_rank = rank(source, source_block, source_row, source_block_row)
    target_rank_row = turn(rank(target, target_block, target_row, target_block_row), 0)
    source_slot = slot_of(lax.bitwise_xor(source_block, mine), odd)
    target_orb_row = sum((target_block_row >= group * i).astype(I32) for i in range(1, orbs))
    outs = list(outs)
    for number, (low, high) in enumerate(phases):
        size = high - low
        extra = group * per_block if number == 0 else 0
        send = outs.pop(0)
        for j in range(orbs):
            to = lax.bitwise_xor(orb, j)
            t = iota((group * size + extra, 1), 0)
            inside = sum((t >= size * i).astype(I32) for i in range(1, group))
            column = slot_of(lax.bitwise_xor(to * group + inside, mine), odd) * size + t - inside * size
            column = jnp.where(t < group * size, column, -1)
            table = jnp.where(column == iota((1, blocks * size), 1), 1.0, 0.0)
            if extra:
                out_row = group * size + (target_block_row - target_orb_row * group) * per_block + target_rank_row
                row_hot = one_hot((t == out_row) & (target_orb_row == to))
                column_hot = one_hot(source_slot * size + source_rank == iota((1, blocks * size), 1))
                table = table + dot(row_hot, column_hot)
            count = group * size + extra
            send[j * count : (j + 1) * count, :] = table.astype(BF16)
    total = group * rows
    w = iota((total, 1), 0)
    inside = sum((w >= rows * i).astype(I32) for i in range(1, group))
    walker = w + orb * total
    first = orb * total + inside * rows
    position, is_target = live_position(walker, first, source_row, target_row, per_block, 1)
    target_before = jnp.sum(((target_row >= first) & (target_row < walker)).astype(I32), axis=1, keepdims=True)
    for number, (low, high) in enumerate(phases):
        size = high - low
        extra = group * per_block if number == 0 else 0
        column = jnp.where((position >= low) & (position < high), inside * size + position - low, -1)
        if extra:
            column = jnp.where(is_target, group * size + inside * per_block + target_before, column)
        outs.pop(0)[...] = one_hot(column == iota((1, group * size + extra), 1))
    local = iota((rows, 1), 0) + mine * rows
    event_hot = one_hot(local == target_row)
    source_hot = one_hot(source_slot * per_block + source_rank == iota((1, blocks * per_block), 1))
    outs.pop(0)[...] = dot(event_hot, source_hot).astype(BF16)


def make_tables(partners, rows, blocks, orbs, per_block, phases):
    group = blocks // orbs
    shapes = []
    extra = [group * per_block] + [0] * (len(phases) - 1)
    for (low, high), more in zip(phases, extra):
        shapes.append((orbs * (group * (high - low) + more), blocks * (high - low)))
    for (low, high), more in zip(phases, extra):
        shapes.append((group * rows, group * (high - low) + more))
    shapes.append((rows, blocks * per_block))
    outs = pl.pallas_call(
        functools.partial(table_kernel, rows, blocks, orbs, per_block, phases),
        in_specs=[VMEM],
        out_specs=[VMEM] * len(shapes),
        out_shape=[jax.ShapeDtypeStruct(s, BF16) for s in shapes],
        compiler_params=params(8),
        cost_estimate=pl.CostEstimate(flops=10_000_000, bytes_accessed=1_000_000, transcendentals=0),
        name="make_tables",
    )(partners)
    n = len(phases)
    return outs[:n], outs[n : 2 * n], outs[2 * n]


def load_kernel(parts, source, out, sem):
    rows = source.shape[0] // parts
    copies = [
        pltpu.make_async_copy(source.at[pl.ds(i * rows, rows)], out.at[pl.ds(i * rows, rows)], sem.at[i])
        for i in range(parts)
    ]
    for copy in copies:
        copy.start()
    for copy in copies:
        copy.wait()


def load(source, parts=8):
    return pl.pallas_call(
        functools.partial(load_kernel, parts),
        in_specs=[HBM],
        out_specs=VMEM,
        out_shape=jax.ShapeDtypeStruct(source.shape, source.dtype),
        scratch_shapes=[pltpu.SemaphoreType.DMA((parts,))],
        compiler_params=params(2),
        cost_estimate=pl.CostEstimate(flops=0, bytes_accessed=2 * source.size, transcendentals=0),
        name="load",
    )(hbm(source))


def contract_kernel(slots, begin, end, offset, tile, turned, has_total, has_table, *refs):
    refs = list(refs)
    pieces = [refs.pop(0) for _ in range(slots)]
    cholesky = refs.pop(0)
    total = refs.pop(0) if has_total else None
    table = refs.pop(0) if has_table else None
    if has_table:
        outs, acc = refs[:-1], refs[-1]
    else:
        acc = refs[0]
    acc[...] = total[...] if has_total else jnp.zeros_like(acc)

    @pl.loop(0, (end - begin) // tile)
    def _(k):
        here = pl.ds(pl.multiple_of(begin + k * tile, tile), tile)
        there = pl.ds(pl.multiple_of(offset + begin + k * tile, tile), tile)
        held = jnp.concatenate([piece[:, here] for piece in pieces], axis=0)
        vectors = cholesky[:, there]
        pair = (vectors, held) if turned else (held, vectors)
        acc[...] += lax.dot_general(*pair, CONTRACT_LAST, preferred_element_type=F32)

    if has_table:
        sent = exact_pick(table[...], acc[...], turned)
        count = sent.shape[0] // len(outs)
        for j, out in enumerate(outs):
            out[...] = sent[j * count : (j + 1) * count]


def contract(pieces, cholesky, begin, end, offset, total, table, orbs, tile, turned):
    size = pieces[0].shape[0]
    rows, vectors = len(pieces) * size, cholesky.shape[0]
    shape = (vectors, rows) if turned else (rows, vectors)
    operands = list(pieces) + [cholesky]
    if total is not None:
        operands.append(total)
    if table is not None:
        operands.append(table)
        out_shape = [jax.ShapeDtypeStruct((table.shape[0] // orbs, vectors), F32)] * orbs
        scratch = [pltpu.VMEM(shape, F32)]
    else:
        out_shape = [jax.ShapeDtypeStruct(shape, F32)]
        scratch = []
    return pl.pallas_call(
        functools.partial(
            contract_kernel, len(pieces), begin, end, offset, tile, turned, total is not None, table is not None
        ),
        in_specs=[VMEM] * len(operands),
        out_specs=[VMEM] * len(out_shape),
        out_shape=out_shape,
        scratch_shapes=scratch,
        compiler_params=params(12),
        cost_estimate=pl.CostEstimate(
            flops=2 * max(rows, 256) * vectors * (end - begin),
            bytes_accessed=2 * vectors * (end - begin),
            transcendentals=0,
        ),
        name="contract",
    )(*operands)


def copy_kernel(slots, parts, per_block, tile, pick, green, *refs):
    pieces, (out, made, sem) = refs[: slots * parts], refs[slots * parts :]
    table = pick[...]
    hit = jnp.max(table.astype(F32), axis=1, keepdims=True) > 0
    copies, at = [], 0
    for part in range(parts):
        here = pieces[part * slots : (part + 1) * slots]
        for t in range(here[0].shape[1] // tile):
            sources = jnp.concatenate([piece[0:per_block, t * tile : (t + 1) * tile] for piece in here], axis=0)
            copied = dot(table, sources).astype(BF16)
            made[:, at : at + tile] = jnp.where(hit, copied, green[:, at : at + tile])
            columns = pl.ds(at, tile)
            copy = pltpu.make_async_copy(made.at[:, columns], out.at[:, columns], sem.at[len(copies)])
            copy.start()
            copies.append(copy)
            at += tile
    for copy in copies:
        copy.wait()


def copy_rows(pick, green, pieces, per_block, tile):
    rows, width = green.shape
    slots = len(pieces[0])
    return pl.pallas_call(
        functools.partial(copy_kernel, slots, len(pieces), per_block, tile),
        in_specs=[VMEM] * (2 + slots * len(pieces)),
        out_specs=HBM,
        out_shape=jax.ShapeDtypeStruct((rows, width), BF16),
        scratch_shapes=[pltpu.VMEM((rows, width), BF16), pltpu.SemaphoreType.DMA((width // tile,))],
        compiler_params=params(8),
        cost_estimate=pl.CostEstimate(flops=2 * rows * 64 * width, bytes_accessed=8 * rows * width, transcendentals=0),
        name="copy_rows",
    )(pick, green, *sum(pieces, []))


def finish_kernel(orbs, groups, has_base, *refs):
    refs = list(refs)
    out = refs.pop()
    result = refs.pop(0)[...] if has_base else None
    for _ in range(groups):
        order = refs.pop(0)[...]
        parts = [refs.pop(0)[...] for _ in range(orbs)]
        term = exact_pick(order, functools.reduce(jnp.add, parts))
        result = term if result is None else result + term
    out[...] = result


def finish(base, groups):
    orbs = len(groups[0][1])
    operands = [] if base is None else [base]
    for order, parts in groups:
        operands += [order, *parts]
    rows, vectors = groups[0][0].shape[0], groups[0][1][0].shape[1]
    return pl.pallas_call(
        functools.partial(finish_kernel, orbs, len(groups), base is not None),
        in_specs=[VMEM] * len(operands),
        out_specs=VMEM,
        out_shape=jax.ShapeDtypeStruct((rows, vectors), F32),
        compiler_params=params(8),
        cost_estimate=pl.CostEstimate(flops=10_000_000, bytes_accessed=1_000_000, transcendentals=0),
        name="finish",
    )(*operands)


def gather_pieces(own, count):
    def send(x, step):
        return lax.ppermute(x, "loop", [(i, i ^ step(i)) for i in range(count)])

    sibling = lambda x: send(x, lambda i: 1)
    ahead = lambda x: send(x, lambda i: 4 if i & 1 else 2)
    aside = lambda x: send(x, lambda i: 2 if i & 1 else 4)
    s0 = sibling(own)
    m1 = ahead(own)
    m2 = ahead(s0)
    f = aside(m1)
    s1 = sibling(m1)
    s2 = sibling(m2)
    s3 = sibling(f)
    return [own, s0, m1, m2, s2, s1, f, s3]


PHASES = ((24, (10, 6)), (16, (8, 8)))
PARTS = 16
CALLS = ((2, 1), (2, 1))
TURNED = (True, True)


def local_phased(cholesky, green_half, partners):
    return phased(cholesky, green_half, partners)


def phased(cholesky, green_half, partners):
    blocks, orbs = lax.axis_size("loop"), lax.axis_size("orb")
    rows, width = green_half.shape
    per_block = partners.shape[0] // blocks
    tile = 1024
    events = partners.T
    spans, phases, low = [], [], 0
    for size, cuts in PHASES:
        left = 0
        for cut in cuts:
            spans.append((low, low + size, left, left + cut * (width // PARTS)))
            left = spans[-1][3]
        phases.append((low, low + size))
        low += size
    own = [None] * len(spans)
    for half in range(2):
        chosen = [i for i, span in enumerate(spans) if (span[2] > 0) == half]
        outs = select_rows(events, green_half, per_block, [spans[i] for i in chosen], 2048)
        for i, out in zip(chosen, outs):
            own[i] = out
    cholesky = load(cholesky)
    sends, orders, pick = make_tables(events, rows, blocks, orbs, per_block, tuple(phases))
    groups, first_pieces, at = [], [], 0
    for number, (size, cuts) in enumerate(PHASES):
        total = None
        for c, cut in enumerate(cuts):
            pieces = gather_pieces(own[at], blocks)
            span = spans[at][3] - spans[at][2]
            calls = CALLS[number][c]
            for k in range(calls):
                last = c == len(cuts) - 1 and k == calls - 1
                begin, end = (span // tile * i // calls * tile for i in (k, k + 1))
                table = sends[number] if last else None
                outs = contract(pieces, cholesky, begin, end, spans[at][2], total, table, orbs, tile, TURNED[number])
                total = outs[0]
            if number == 0:
                first_pieces.append(pieces)
            at += 1
        parts = [outs[0]]
        for j in range(orbs - 1, 0, -1):
            parts.append(lax.ppermute(outs[j], "orb", [(i, i ^ j) for i in range(orbs)]))
        groups.append((orders[number], parts))
    new_green = copy_rows(pick, green_half, first_pieces, per_block, 2 * tile)
    base = finish(None, groups[:-1])
    return new_green, finish(base, groups[-1:])


def contract_plain(shard_rows, cholesky):
    return lax.dot_general(shard_rows, cholesky, CONTRACT_LAST, preferred_element_type=F32)


def local_gathered(cholesky, green_half, partners):
    loop_count = lax.axis_size("loop")
    block_rows = green_half.shape[0]
    walkers = block_rows * loop_count
    per_block = partners.shape[0] // loop_count
    sources, targets = partners[:, 0], partners[:, 1]
    first_row = lax.axis_index("loop") * block_rows
    walker_index = jnp.arange(walkers, dtype=I32)
    hits = targets[None, :] == walker_index[:, None]
    overwritten = jnp.any(hits, axis=1)
    anchor = jnp.where(overwritten, jnp.sum(jnp.where(hits, sources[None, :], 0), axis=1), walker_index)
    local_flags = lax.dynamic_slice_in_dim(overwritten, first_row, block_rows)
    local_targets = jnp.nonzero(local_flags, size=per_block)[0].astype(I32)
    local_anchor = jnp.take(anchor, first_row + local_targets)
    shard_rows = lax.all_gather(green_half, "loop", axis=0, tiled=True)
    bias = contract_plain(shard_rows, cholesky)
    select = (local_anchor[:, None] == walker_index[None, :]).astype(BF16)
    copied = dot(select, shard_rows).astype(BF16)
    new_green = green_half.at[local_targets].set(copied)
    full_bias = jnp.take(bias, anchor, axis=0)
    return new_green, lax.psum_scatter(full_bias, "orb", scatter_dimension=0, tiled=True)


def solution(mesh):
    blocks, orbs = mesh.shape["loop"], mesh.shape["orb"]
    cube = blocks == 2**3 and orbs == 2**2
    return jax.shard_map(
        local_phased if cube else local_gathered,
        mesh=mesh,
        in_specs=(P("loop", "orb"), P("loop", "orb"), P()),
        out_specs=(P("loop", "orb"), P("orb", "loop")),
        check_vma=False,
    )
```

```python
import functools

import jax
import jax.numpy as jnp
from jax import lax
from jax.experimental import pallas as pl
from jax.experimental.pallas import tpu as pltpu
from jax.sharding import PartitionSpec as P


VMEM = pl.BlockSpec(memory_space=pltpu.VMEM)
HBM = pl.BlockSpec(memory_space=pltpu.HBM)
I32 = jnp.int32
F32 = jnp.float32
BF16 = jnp.bfloat16
CONTRACT_LAST = (((1,), (1,)), ((), ()))


def iota(shape, axis):
    return lax.broadcasted_iota(I32, shape, axis)


def one_hot(condition):
    return jnp.where(condition, 1.0, 0.0).astype(BF16)


def turn(line, axis):
    count = max(line.shape)
    eye = iota((count, count), 0) == iota((count, count), 1)
    return jnp.sum(jnp.where(eye, line, 0), axis=axis, keepdims=True)


def dot(a, b):
    return jnp.dot(a, b, preferred_element_type=F32)


def exact_pick(select, values, turned=False):
    high = values.astype(BF16)
    rest = values - high.astype(F32)
    middle = rest.astype(BF16)
    low = (rest - middle.astype(F32)).astype(BF16)
    numbers = CONTRACT_LAST if turned else (((1,), (0,)), ((), ()))
    take = lambda piece: lax.dot_general(select, piece, numbers, preferred_element_type=F32)
    return take(high) + take(middle) + take(low)


def hbm(x):
    return pltpu.with_memory_space_constraint(x, pltpu.HBM)


def params(megabytes=None, **kw):
    if megabytes is not None:
        kw["vmem_limit_bytes"] = megabytes << 20
    return pltpu.CompilerParams(**kw)


def slot_of(offset, odd):
    swapped = jnp.where((offset == 2) | (offset == 3), offset + 2, jnp.where((offset == 4) | (offset == 5), offset - 2, offset))
    return jnp.where(odd == 1, swapped, offset)


def live_position(walker, first, sources, targets, per_block, axis):
    count = lambda condition: jnp.sum(condition.astype(I32), axis=axis, keepdims=True)
    is_source = count(sources == walker) > 0
    is_target = count(targets == walker) > 0
    sources_before = count((sources >= first) & (sources < walker))
    targets_before = count((targets >= first) & (targets < walker))
    plain = per_block + walker - first - sources_before - targets_before
    return jnp.where(is_target, -1, jnp.where(is_source, sources_before, plain)), is_target


def select_kernel(per_block, spans, begin, tile, events, green, *refs):
    outs, (partners, held, event_sem, sem) = refs[: len(spans)], refs[len(spans) :]
    fetch = pltpu.make_async_copy(events, partners, event_sem)
    fetch.start()
    rows, width = held.shape
    tiles = width // tile
    copies = [
        pltpu.make_async_copy(
            green.at[:, pl.ds(begin + t * tile, tile)], held.at[:, pl.ds(t * tile, tile)], sem.at[t]
        )
        for t in range(tiles)
    ]
    for copy in copies:
        copy.start()
    first = lax.axis_index("loop") * rows
    fetch.wait()
    source, target = turn(partners[0:1, :], 1), turn(partners[1:2, :], 1)
    walker = iota((1, rows), 1) + first
    position, _ = live_position(walker, first, source, target, per_block, 0)
    live = rows - per_block
    select = one_hot(iota((live, rows), 0) == position)
    for t in range(tiles):
        copies[t].wait()
        picked = dot(select, held[:, t * tile : (t + 1) * tile]).astype(BF16)
        for out, (low, high, left, right) in zip(outs, spans):
            at = begin + t * tile
            if left <= at < right:
                out[:, at - left : at - left + tile] = picked[low:high]


def select_rows(partners, green, per_block, spans, tile):
    rows, begin = green.shape[0], min(span[2] for span in spans)
    width = max(span[3] for span in spans) - begin
    return pl.pallas_call(
        functools.partial(select_kernel, per_block, spans, begin, tile),
        in_specs=[HBM, HBM],
        out_specs=[VMEM] * len(spans),
        out_shape=[jax.ShapeDtypeStruct((h - l, b - a), BF16) for l, h, a, b in spans],
        scratch_shapes=[
            pltpu.VMEM(partners.shape, I32),
            pltpu.VMEM((rows, width), BF16),
            pltpu.SemaphoreType.DMA,
            pltpu.SemaphoreType.DMA((width // tile,)),
        ],
        compiler_params=params(8),
        cost_estimate=pl.CostEstimate(flops=2 * rows * rows * width, bytes_accessed=4 * rows * width, transcendentals=0),
        name="select_rows",
    )(hbm(partners), hbm(green))


def table_kernel(rows, blocks, orbs, per_block, phases, partners, *outs):
    mine, orb = lax.axis_index("loop"), lax.axis_index("orb")
    odd = lax.bitwise_and(mine, 1)
    group = blocks // orbs
    source_row, target_row = partners[0:1, :], partners[1:2, :]
    source, target = turn(source_row, 1), turn(target_row, 1)
    block_of = lambda walker: sum((walker >= rows * i).astype(I32) for i in range(1, blocks))
    source_block, target_block = block_of(source), block_of(target)
    source_block_row, target_block_row = block_of(source_row), block_of(target_row)
    rank = lambda own, own_block, other, other_block: jnp.sum(
        ((own_block == other_block) & (other < own)).astype(I32), axis=1, keepdims=True
    )
    source_rank = rank(source, source_block, source_row, source_block_row)
    target_rank_row = turn(rank(target, target_block, target_row, target_block_row), 0)
    source_slot = slot_of(lax.bitwise_xor(source_block, mine), odd)
    target_orb_row = sum((target_block_row >= group * i).astype(I32) for i in range(1, orbs))
    outs = list(outs)
    for number, (low, high) in enumerate(phases):
        size = high - low
        extra = group * per_block if number == 0 else 0
        send = outs.pop(0)
        for j in range(orbs):
            to = lax.bitwise_xor(orb, j)
            t = iota((group * size + extra, 1), 0)
            inside = sum((t >= size * i).astype(I32) for i in range(1, group))
            column = slot_of(lax.bitwise_xor(to * group + inside, mine), odd) * size + t - inside * size
            column = jnp.where(t < group * size, column, -1)
            table = jnp.where(column == iota((1, blocks * size), 1), 1.0, 0.0)
            if extra:
                out_row = group * size + (target_block_row - target_orb_row * group) * per_block + target_rank_row
                row_hot = one_hot((t == out_row) & (target_orb_row == to))
                column_hot = one_hot(source_slot * size + source_rank == iota((1, blocks * size), 1))
                table = table + dot(row_hot, column_hot)
            count = group * size + extra
            send[j * count : (j + 1) * count, :] = table.astype(BF16)
    total = group * rows
    w = iota((total, 1), 0)
    inside = sum((w >= rows * i).astype(I32) for i in range(1, group))
    walker = w + orb * total
    first = orb * total + inside * rows
    position, is_target = live_position(walker, first, source_row, target_row, per_block, 1)
    target_before = jnp.sum(((target_row >= first) & (target_row < walker)).astype(I32), axis=1, keepdims=True)
    for number, (low, high) in enumerate(phases):
        size = high - low
        extra = group * per_block if number == 0 else 0
        column = jnp.where((position >= low) & (position < high), inside * size + position - low, -1)
        if extra:
            column = jnp.where(is_target, group * size + inside * per_block + target_before, column)
        outs.pop(0)[...] = one_hot(column == iota((1, group * size + extra), 1))
    local = iota((rows, 1), 0) + mine * rows
    event_hot = one_hot(local == target_row)
    source_hot = one_hot(source_slot * per_block + source_rank == iota((1, blocks * per_block), 1))
    outs.pop(0)[...] = dot(event_hot, source_hot).astype(BF16)


def make_tables(partners, rows, blocks, orbs, per_block, phases):
    group = blocks // orbs
    shapes = []
    extra = [group * per_block] + [0] * (len(phases) - 1)
    for (low, high), more in zip(phases, extra):
        shapes.append((orbs * (group * (high - low) + more), blocks * (high - low)))
    for (low, high), more in zip(phases, extra):
        shapes.append((group * rows, group * (high - low) + more))
    shapes.append((rows, blocks * per_block))
    outs = pl.pallas_call(
        functools.partial(table_kernel, rows, blocks, orbs, per_block, phases),
        in_specs=[VMEM],
        out_specs=[VMEM] * len(shapes),
        out_shape=[jax.ShapeDtypeStruct(s, BF16) for s in shapes],
        compiler_params=params(8),
        cost_estimate=pl.CostEstimate(flops=10_000_000, bytes_accessed=1_000_000, transcendentals=0),
        name="make_tables",
    )(partners)
    n = len(phases)
    return outs[:n], outs[n : 2 * n], outs[2 * n]


def load_kernel(parts, source, out, sem):
    rows = source.shape[0] // parts
    copies = [
        pltpu.make_async_copy(source.at[pl.ds(i * rows, rows)], out.at[pl.ds(i * rows, rows)], sem.at[i])
        for i in range(parts)
    ]
    for copy in copies:
        copy.start()
    for copy in copies:
        copy.wait()


def load(source, parts=8):
    return pl.pallas_call(
        functools.partial(load_kernel, parts),
        in_specs=[HBM],
        out_specs=VMEM,
        out_shape=jax.ShapeDtypeStruct(source.shape, source.dtype),
        scratch_shapes=[pltpu.SemaphoreType.DMA((parts,))],
        compiler_params=params(2),
        cost_estimate=pl.CostEstimate(flops=0, bytes_accessed=2 * source.size, transcendentals=0),
        name="load",
    )(hbm(source))


def contract_kernel(slots, begin, end, offset, tile, turned, has_total, has_table, *refs):
    refs = list(refs)
    pieces = [refs.pop(0) for _ in range(slots)]
    cholesky = refs.pop(0)
    total = refs.pop(0) if has_total else None
    table = refs.pop(0) if has_table else None
    if has_table:
        outs, acc = refs[:-1], refs[-1]
    else:
        acc = refs[0]
    acc[...] = total[...] if has_total else jnp.zeros_like(acc)

    @pl.loop(0, (end - begin) // tile, unroll=True)
    def _(k):
        here = pl.ds(pl.multiple_of(begin + k * tile, tile), tile)
        there = pl.ds(pl.multiple_of(offset + begin + k * tile, tile), tile)
        held = jnp.concatenate([piece[:, here] for piece in pieces], axis=0)
        vectors = cholesky[:, there]
        pair = (vectors, held) if turned else (held, vectors)
        acc[...] += lax.dot_general(*pair, CONTRACT_LAST, preferred_element_type=F32)

    if has_table:
        sent = exact_pick(table[...], acc[...], turned)
        count = sent.shape[0] // len(outs)
        for j, out in enumerate(outs):
            out[...] = sent[j * count : (j + 1) * count]


def contract(pieces, cholesky, begin, end, offset, total, table, orbs, tile, turned):
    size = pieces[0].shape[0]
    rows, vectors = len(pieces) * size, cholesky.shape[0]
    shape = (vectors, rows) if turned else (rows, vectors)
    operands = list(pieces) + [cholesky]
    if total is not None:
        operands.append(total)
    if table is not None:
        operands.append(table)
        out_shape = [jax.ShapeDtypeStruct((table.shape[0] // orbs, vectors), F32)] * orbs
        scratch = [pltpu.VMEM(shape, F32)]
    else:
        out_shape = [jax.ShapeDtypeStruct(shape, F32)]
        scratch = []
    return pl.pallas_call(
        functools.partial(
            contract_kernel, len(pieces), begin, end, offset, tile, turned, total is not None, table is not None
        ),
        in_specs=[VMEM] * len(operands),
        out_specs=[VMEM] * len(out_shape),
        out_shape=out_shape,
        scratch_shapes=scratch,
        compiler_params=params(12),
        cost_estimate=pl.CostEstimate(
            flops=2 * max(rows, 256) * vectors * (end - begin),
            bytes_accessed=2 * vectors * (end - begin),
            transcendentals=0,
        ),
        name="contract",
    )(*operands)


def copy_kernel(slots, parts, per_block, tile, pick, green, *refs):
    pieces, (out, made, sem) = refs[: slots * parts], refs[slots * parts :]
    table = pick[...]
    hit = jnp.max(table.astype(F32), axis=1, keepdims=True) > 0
    copies, at = [], 0
    for part in range(parts):
        here = pieces[part * slots : (part + 1) * slots]
        for t in range(here[0].shape[1] // tile):
            sources = jnp.concatenate([piece[0:per_block, t * tile : (t + 1) * tile] for piece in here], axis=0)
            copied = dot(table, sources).astype(BF16)
            made[:, at : at + tile] = jnp.where(hit, copied, green[:, at : at + tile])
            columns = pl.ds(at, tile)
            copy = pltpu.make_async_copy(made.at[:, columns], out.at[:, columns], sem.at[len(copies)])
            copy.start()
            copies.append(copy)
            at += tile
    for copy in copies:
        copy.wait()


def copy_rows(pick, green, pieces, per_block, tile):
    rows, width = green.shape
    slots = len(pieces[0])
    return pl.pallas_call(
        functools.partial(copy_kernel, slots, len(pieces), per_block, tile),
        in_specs=[VMEM] * (2 + slots * len(pieces)),
        out_specs=HBM,
        out_shape=jax.ShapeDtypeStruct((rows, width), BF16),
        scratch_shapes=[pltpu.VMEM((rows, width), BF16), pltpu.SemaphoreType.DMA((width // tile,))],
        compiler_params=params(8),
        cost_estimate=pl.CostEstimate(flops=2 * rows * 64 * width, bytes_accessed=8 * rows * width, transcendentals=0),
        name="copy_rows",
    )(pick, green, *sum(pieces, []))


def finish_kernel(orbs, groups, has_base, *refs):
    refs = list(refs)
    out = refs.pop()
    result = refs.pop(0)[...] if has_base else None
    for _ in range(groups):
        order = refs.pop(0)[...]
        parts = [refs.pop(0)[...] for _ in range(orbs)]
        term = exact_pick(order, functools.reduce(jnp.add, parts))
        result = term if result is None else result + term
    out[...] = result


def finish(base, groups):
    orbs = len(groups[0][1])
    operands = [] if base is None else [base]
    for order, parts in groups:
        operands += [order, *parts]
    rows, vectors = groups[0][0].shape[0], groups[0][1][0].shape[1]
    return pl.pallas_call(
        functools.partial(finish_kernel, orbs, len(groups), base is not None),
        in_specs=[VMEM] * len(operands),
        out_specs=VMEM,
        out_shape=jax.ShapeDtypeStruct((rows, vectors), F32),
        compiler_params=params(8),
        cost_estimate=pl.CostEstimate(flops=10_000_000, bytes_accessed=1_000_000, transcendentals=0),
        name="finish",
    )(*operands)


def gather_pieces(own, count):
    def send(x, step):
        return lax.ppermute(x, "loop", [(i, i ^ step(i)) for i in range(count)])

    sibling = lambda x: send(x, lambda i: 1)
    ahead = lambda x: send(x, lambda i: 4 if i & 1 else 2)
    aside = lambda x: send(x, lambda i: 2 if i & 1 else 4)
    s0 = sibling(own)
    m1 = ahead(own)
    m2 = ahead(s0)
    f = aside(m1)
    s1 = sibling(m1)
    s2 = sibling(m2)
    s3 = sibling(f)
    return [own, s0, m1, m2, s2, s1, f, s3]


PHASES = ((24, (8, 8)), (16, (10, 6)))
PARTS = 16
CALLS = ((1, 2), (2, 1))
TURNED = (True, True)


def local_phased(cholesky, green_half, partners):
    return phased(cholesky, green_half, partners)


def phased(cholesky, green_half, partners):
    blocks, orbs = lax.axis_size("loop"), lax.axis_size("orb")
    rows, width = green_half.shape
    per_block = partners.shape[0] // blocks
    tile = 1024
    events = partners.T
    spans, phases, low = [], [], 0
    for size, cuts in PHASES:
        left = 0
        for cut in cuts:
            spans.append((low, low + size, left, left + cut * (width // PARTS)))
            left = spans[-1][3]
        phases.append((low, low + size))
        low += size
    own = [None] * len(spans)
    for half in range(2):
        chosen = [i for i, span in enumerate(spans) if (span[2] > 0) == half]
        outs = select_rows(events, green_half, per_block, [spans[i] for i in chosen], 2048)
        for i, out in zip(chosen, outs):
            own[i] = out
    cholesky = load(cholesky)
    sends, orders, pick = make_tables(events, rows, blocks, orbs, per_block, tuple(phases))
    groups, first_pieces, at = [], [], 0
    for number, (size, cuts) in enumerate(PHASES):
        total = None
        for c, cut in enumerate(cuts):
            pieces = gather_pieces(own[at], blocks)
            span = spans[at][3] - spans[at][2]
            calls = CALLS[number][c]
            for k in range(calls):
                last = c == len(cuts) - 1 and k == calls - 1
                begin, end = (span // tile * i // calls * tile for i in (k, k + 1))
                table = sends[number] if last else None
                outs = contract(pieces, cholesky, begin, end, spans[at][2], total, table, orbs, tile, TURNED[number])
                total = outs[0]
            if number == 0:
                first_pieces.append(pieces)
            at += 1
        parts = [outs[0]]
        for j in range(orbs - 1, 0, -1):
            parts.append(lax.ppermute(outs[j], "orb", [(i, i ^ j) for i in range(orbs)]))
        groups.append((orders[number], parts))
    new_green = copy_rows(pick, green_half, first_pieces, per_block, 2 * tile)
    base = finish(None, groups[:-1])
    return new_green, finish(base, groups[-1:])


def contract_plain(shard_rows, cholesky):
    return lax.dot_general(shard_rows, cholesky, CONTRACT_LAST, preferred_element_type=F32)


def local_gathered(cholesky, green_half, partners):
    loop_count = lax.axis_size("loop")
    block_rows = green_half.shape[0]
    walkers = block_rows * loop_count
    per_block = partners.shape[0] // loop_count
    sources, targets = partners[:, 0], partners[:, 1]
    first_row = lax.axis_index("loop") * block_rows
    walker_index = jnp.arange(walkers, dtype=I32)
    hits = targets[None, :] == walker_index[:, None]
    overwritten = jnp.any(hits, axis=1)
    anchor = jnp.where(overwritten, jnp.sum(jnp.where(hits, sources[None, :], 0), axis=1), walker_index)
    local_flags = lax.dynamic_slice_in_dim(overwritten, first_row, block_rows)
    local_targets = jnp.nonzero(local_flags, size=per_block)[0].astype(I32)
    local_anchor = jnp.take(anchor, first_row + local_targets)
    shard_rows = lax.all_gather(green_half, "loop", axis=0, tiled=True)
    bias = contract_plain(shard_rows, cholesky)
    select = (local_anchor[:, None] == walker_index[None, :]).astype(BF16)
    copied = dot(select, shard_rows).astype(BF16)
    new_green = green_half.at[local_targets].set(copied)
    full_bias = jnp.take(bias, anchor, axis=0)
    return new_green, lax.psum_scatter(full_bias, "orb", scatter_dimension=0, tiled=True)


def solution(mesh):
    blocks, orbs = mesh.shape["loop"], mesh.shape["orb"]
    cube = blocks == 2**3 and orbs == 2**2
    return jax.shard_map(
        local_phased if cube else local_gathered,
        mesh=mesh,
        in_specs=(P("loop", "orb"), P("loop", "orb"), P()),
        out_specs=(P("loop", "orb"), P("orb", "loop")),
        check_vma=False,
    )
```

```python
import functools

import jax
import jax.numpy as jnp
from jax import lax
from jax.experimental import pallas as pl
from jax.experimental.pallas import tpu as pltpu
from jax.sharding import PartitionSpec as P


VMEM = pl.BlockSpec(memory_space=pltpu.VMEM)
HBM = pl.BlockSpec(memory_space=pltpu.HBM)
I32 = jnp.int32
F32 = jnp.float32
BF16 = jnp.bfloat16
CONTRACT_LAST = (((1,), (1,)), ((), ()))


def iota(shape, axis):
    return lax.broadcasted_iota(I32, shape, axis)


def one_hot(condition):
    return jnp.where(condition, 1.0, 0.0).astype(BF16)


def turn(line, axis):
    count = max(line.shape)
    eye = iota((count, count), 0) == iota((count, count), 1)
    return jnp.sum(jnp.where(eye, line, 0), axis=axis, keepdims=True)


def dot(a, b):
    return jnp.dot(a, b, preferred_element_type=F32)


def exact_pick(select, values, turned=False):
    high = values.astype(BF16)
    rest = values - high.astype(F32)
    middle = rest.astype(BF16)
    low = (rest - middle.astype(F32)).astype(BF16)
    numbers = CONTRACT_LAST if turned else (((1,), (0,)), ((), ()))
    take = lambda piece: lax.dot_general(select, piece, numbers, preferred_element_type=F32)
    return take(high) + take(middle) + take(low)


def hbm(x):
    return pltpu.with_memory_space_constraint(x, pltpu.HBM)


def params(megabytes=None, **kw):
    if megabytes is not None:
        kw["vmem_limit_bytes"] = megabytes << 20
    return pltpu.CompilerParams(**kw)


def slot_of(offset, odd):
    swapped = jnp.where((offset == 2) | (offset == 3), offset + 2, jnp.where((offset == 4) | (offset == 5), offset - 2, offset))
    return jnp.where(odd == 1, swapped, offset)


def live_position(walker, first, sources, targets, per_block, axis):
    count = lambda condition: jnp.sum(condition.astype(I32), axis=axis, keepdims=True)
    is_source = count(sources == walker) > 0
    is_target = count(targets == walker) > 0
    sources_before = count((sources >= first) & (sources < walker))
    targets_before = count((targets >= first) & (targets < walker))
    plain = per_block + walker - first - sources_before - targets_before
    return jnp.where(is_target, -1, jnp.where(is_source, sources_before, plain)), is_target


def select_kernel(per_block, spans, begin, tile, events, green, *refs):
    outs, (partners, held, event_sem, sem) = refs[: len(spans)], refs[len(spans) :]
    fetch = pltpu.make_async_copy(events, partners, event_sem)
    fetch.start()
    rows, width = held.shape
    tiles = width // tile
    copies = [
        pltpu.make_async_copy(
            green.at[:, pl.ds(begin + t * tile, tile)], held.at[:, pl.ds(t * tile, tile)], sem.at[t]
        )
        for t in range(tiles)
    ]
    for copy in copies:
        copy.start()
    first = lax.axis_index("loop") * rows
    fetch.wait()
    source, target = turn(partners[0:1, :], 1), turn(partners[1:2, :], 1)
    walker = iota((1, rows), 1) + first
    position, _ = live_position(walker, first, source, target, per_block, 0)
    live = rows - per_block
    select = one_hot(iota((live, rows), 0) == position)
    for t in range(tiles):
        copies[t].wait()
        picked = dot(select, held[:, t * tile : (t + 1) * tile]).astype(BF16)
        for out, (low, high, left, right) in zip(outs, spans):
            at = begin + t * tile
            if left <= at < right:
                out[:, at - left : at - left + tile] = picked[low:high]


def select_rows(partners, green, per_block, spans, tile):
    rows, begin = green.shape[0], min(span[2] for span in spans)
    width = max(span[3] for span in spans) - begin
    return pl.pallas_call(
        functools.partial(select_kernel, per_block, spans, begin, tile),
        in_specs=[HBM, HBM],
        out_specs=[VMEM] * len(spans),
        out_shape=[jax.ShapeDtypeStruct((h - l, b - a), BF16) for l, h, a, b in spans],
        scratch_shapes=[
            pltpu.VMEM(partners.shape, I32),
            pltpu.VMEM((rows, width), BF16),
            pltpu.SemaphoreType.DMA,
            pltpu.SemaphoreType.DMA((width // tile,)),
        ],
        compiler_params=params(8),
        cost_estimate=pl.CostEstimate(flops=2 * rows * rows * width, bytes_accessed=4 * rows * width, transcendentals=0),
        name="select_rows",
    )(hbm(partners), hbm(green))


def table_kernel(rows, blocks, orbs, per_block, phases, partners, *outs):
    mine, orb = lax.axis_index("loop"), lax.axis_index("orb")
    odd = lax.bitwise_and(mine, 1)
    group = blocks // orbs
    source_row, target_row = partners[0:1, :], partners[1:2, :]
    source, target = turn(source_row, 1), turn(target_row, 1)
    block_of = lambda walker: sum((walker >= rows * i).astype(I32) for i in range(1, blocks))
    source_block, target_block = block_of(source), block_of(target)
    source_block_row, target_block_row = block_of(source_row), block_of(target_row)
    rank = lambda own, own_block, other, other_block: jnp.sum(
        ((own_block == other_block) & (other < own)).astype(I32), axis=1, keepdims=True
    )
    source_rank = rank(source, source_block, source_row, source_block_row)
    target_rank_row = turn(rank(target, target_block, target_row, target_block_row), 0)
    source_slot = slot_of(lax.bitwise_xor(source_block, mine), odd)
    target_orb_row = sum((target_block_row >= group * i).astype(I32) for i in range(1, orbs))
    outs = list(outs)
    for number, (low, high) in enumerate(phases):
        size = high - low
        extra = group * per_block if number == 0 else 0
        send = outs.pop(0)
        for j in range(orbs):
            to = lax.bitwise_xor(orb, j)
            t = iota((group * size + extra, 1), 0)
            inside = sum((t >= size * i).astype(I32) for i in range(1, group))
            column = slot_of(lax.bitwise_xor(to * group + inside, mine), odd) * size + t - inside * size
            column = jnp.where(t < group * size, column, -1)
            table = jnp.where(column == iota((1, blocks * size), 1), 1.0, 0.0)
            if extra:
                out_row = group * size + (target_block_row - target_orb_row * group) * per_block + target_rank_row
                row_hot = one_hot((t == out_row) & (target_orb_row == to))
                column_hot = one_hot(source_slot * size + source_rank == iota((1, blocks * size), 1))
                table = table + dot(row_hot, column_hot)
            count = group * size + extra
            send[j * count : (j + 1) * count, :] = table.astype(BF16)
    total = group * rows
    w = iota((total, 1), 0)
    inside = sum((w >= rows * i).astype(I32) for i in range(1, group))
    walker = w + orb * total
    first = orb * total + inside * rows
    position, is_target = live_position(walker, first, source_row, target_row, per_block, 1)
    target_before = jnp.sum(((target_row >= first) & (target_row < walker)).astype(I32), axis=1, keepdims=True)
    for number, (low, high) in enumerate(phases):
        size = high - low
        extra = group * per_block if number == 0 else 0
        column = jnp.where((position >= low) & (position < high), inside * size + position - low, -1)
        if extra:
            column = jnp.where(is_target, group * size + inside * per_block + target_before, column)
        outs.pop(0)[...] = one_hot(column == iota((1, group * size + extra), 1))
    local = iota((rows, 1), 0) + mine * rows
    event_hot = one_hot(local == target_row)
    source_hot = one_hot(source_slot * per_block + source_rank == iota((1, blocks * per_block), 1))
    outs.pop(0)[...] = dot(event_hot, source_hot).astype(BF16)


def make_tables(partners, rows, blocks, orbs, per_block, phases):
    group = blocks // orbs
    shapes = []
    extra = [group * per_block] + [0] * (len(phases) - 1)
    for (low, high), more in zip(phases, extra):
        shapes.append((orbs * (group * (high - low) + more), blocks * (high - low)))
    for (low, high), more in zip(phases, extra):
        shapes.append((group * rows, group * (high - low) + more))
    shapes.append((rows, blocks * per_block))
    outs = pl.pallas_call(
        functools.partial(table_kernel, rows, blocks, orbs, per_block, phases),
        in_specs=[VMEM],
        out_specs=[VMEM] * len(shapes),
        out_shape=[jax.ShapeDtypeStruct(s, BF16) for s in shapes],
        compiler_params=params(8),
        cost_estimate=pl.CostEstimate(flops=10_000_000, bytes_accessed=1_000_000, transcendentals=0),
        name="make_tables",
    )(partners)
    n = len(phases)
    return outs[:n], outs[n : 2 * n], outs[2 * n]


def load_kernel(parts, source, out, sem):
    rows = source.shape[0] // parts
    copies = [
        pltpu.make_async_copy(source.at[pl.ds(i * rows, rows)], out.at[pl.ds(i * rows, rows)], sem.at[i])
        for i in range(parts)
    ]
    for copy in copies:
        copy.start()
    for copy in copies:
        copy.wait()


def load(source, parts=8):
    return pl.pallas_call(
        functools.partial(load_kernel, parts),
        in_specs=[HBM],
        out_specs=VMEM,
        out_shape=jax.ShapeDtypeStruct(source.shape, source.dtype),
        scratch_shapes=[pltpu.SemaphoreType.DMA((parts,))],
        compiler_params=params(2),
        cost_estimate=pl.CostEstimate(flops=0, bytes_accessed=2 * source.size, transcendentals=0),
        name="load",
    )(hbm(source))


def contract_kernel(slots, begin, end, offset, tile, turned, has_total, has_table, *refs):
    refs = list(refs)
    pieces = [refs.pop(0) for _ in range(slots)]
    cholesky = refs.pop(0)
    total = refs.pop(0) if has_total else None
    table = refs.pop(0) if has_table else None
    if has_table:
        outs, acc = refs[:-1], refs[-1]
    else:
        acc = refs[0]
    acc[...] = total[...] if has_total else jnp.zeros_like(acc)

    @pl.loop(0, (end - begin) // tile, unroll=True)
    def _(k):
        here = pl.ds(pl.multiple_of(begin + k * tile, tile), tile)
        there = pl.ds(pl.multiple_of(offset + begin + k * tile, tile), tile)
        held = jnp.concatenate([piece[:, here] for piece in pieces], axis=0)
        vectors = cholesky[:, there]
        pair = (vectors, held) if turned else (held, vectors)
        acc[...] += lax.dot_general(*pair, CONTRACT_LAST, preferred_element_type=F32)

    if has_table:
        sent = exact_pick(table[...], acc[...], turned)
        count = sent.shape[0] // len(outs)
        for j, out in enumerate(outs):
            out[...] = sent[j * count : (j + 1) * count]


def contract(pieces, cholesky, begin, end, offset, total, table, orbs, tile, turned):
    size = pieces[0].shape[0]
    rows, vectors = len(pieces) * size, cholesky.shape[0]
    shape = (vectors, rows) if turned else (rows, vectors)
    operands = list(pieces) + [cholesky]
    if total is not None:
        operands.append(total)
    if table is not None:
        operands.append(table)
        out_shape = [jax.ShapeDtypeStruct((table.shape[0] // orbs, vectors), F32)] * orbs
        scratch = [pltpu.VMEM(shape, F32)]
    else:
        out_shape = [jax.ShapeDtypeStruct(shape, F32)]
        scratch = []
    return pl.pallas_call(
        functools.partial(
            contract_kernel, len(pieces), begin, end, offset, tile, turned, total is not None, table is not None
        ),
        in_specs=[VMEM] * len(operands),
        out_specs=[VMEM] * len(out_shape),
        out_shape=out_shape,
        scratch_shapes=scratch,
        compiler_params=params(12),
        cost_estimate=pl.CostEstimate(
            flops=2 * max(rows, 256) * vectors * (end - begin),
            bytes_accessed=2 * vectors * (end - begin),
            transcendentals=0,
        ),
        name="contract",
    )(*operands)


def copy_kernel(slots, parts, per_block, tile, pick, green, *refs):
    pieces, (out, made, sem) = refs[: slots * parts], refs[slots * parts :]
    table = pick[...]
    hit = jnp.max(table.astype(F32), axis=1, keepdims=True) > 0
    copies, at = [], 0
    for part in range(parts):
        here = pieces[part * slots : (part + 1) * slots]
        for t in range(here[0].shape[1] // tile):
            sources = jnp.concatenate([piece[0:per_block, t * tile : (t + 1) * tile] for piece in here], axis=0)
            copied = dot(table, sources).astype(BF16)
            made[:, at : at + tile] = jnp.where(hit, copied, green[:, at : at + tile])
            columns = pl.ds(at, tile)
            copy = pltpu.make_async_copy(made.at[:, columns], out.at[:, columns], sem.at[len(copies)])
            copy.start()
            copies.append(copy)
            at += tile
    for copy in copies:
        copy.wait()


def copy_rows(pick, green, pieces, per_block, tile):
    rows, width = green.shape
    slots = len(pieces[0])
    return pl.pallas_call(
        functools.partial(copy_kernel, slots, len(pieces), per_block, tile),
        in_specs=[VMEM] * (2 + slots * len(pieces)),
        out_specs=HBM,
        out_shape=jax.ShapeDtypeStruct((rows, width), BF16),
        scratch_shapes=[pltpu.VMEM((rows, width), BF16), pltpu.SemaphoreType.DMA((width // tile,))],
        compiler_params=params(8),
        cost_estimate=pl.CostEstimate(flops=2 * rows * 64 * width, bytes_accessed=8 * rows * width, transcendentals=0),
        name="copy_rows",
    )(pick, green, *sum(pieces, []))


def finish_kernel(orbs, groups, has_base, cuts, *refs):
    refs = list(refs)
    out, made, sem = refs[-3:] if cuts else (refs[-1], refs[-1], None)
    base = refs.pop(0) if has_base else None
    terms = []
    for _ in range(groups):
        order = refs.pop(0)
        parts = [refs.pop(0)[...] for _ in range(orbs)]
        terms.append((order, functools.reduce(jnp.add, parts)))
    rows = made.shape[0] // max(cuts, 1)
    copies = []
    for i in range(max(cuts, 1)):
        here = slice(i * rows, (i + 1) * rows)
        picked = [exact_pick(order[here, :], total) for order, total in terms]
        if has_base:
            picked.insert(0, base[here, :])
        made[here, :] = functools.reduce(jnp.add, picked)
        if cuts:
            copies.append(pltpu.make_async_copy(made.at[here], out.at[here], sem.at[i]))
            copies[-1].start()
    for copy in copies:
        copy.wait()


def finish(base, groups, cuts=0):
    orbs = len(groups[0][1])
    operands = [] if base is None else [base]
    for order, parts in groups:
        operands += [order, *parts]
    rows, vectors = groups[0][0].shape[0], groups[0][1][0].shape[1]
    scratch = [pltpu.VMEM((rows, vectors), F32), pltpu.SemaphoreType.DMA((cuts,))] if cuts else []
    return pl.pallas_call(
        functools.partial(finish_kernel, orbs, len(groups), base is not None, cuts),
        in_specs=[VMEM] * len(operands),
        out_specs=HBM if cuts else VMEM,
        out_shape=jax.ShapeDtypeStruct((rows, vectors), F32),
        scratch_shapes=scratch,
        compiler_params=params(8),
        cost_estimate=pl.CostEstimate(flops=10_000_000, bytes_accessed=1_000_000, transcendentals=0),
        name="finish",
    )(*operands)


def gather_pieces(own, count):
    def send(x, step):
        return lax.ppermute(x, "loop", [(i, i ^ step(i)) for i in range(count)])

    sibling = lambda x: send(x, lambda i: 1)
    ahead = lambda x: send(x, lambda i: 4 if i & 1 else 2)
    aside = lambda x: send(x, lambda i: 2 if i & 1 else 4)
    s0 = sibling(own)
    m1 = ahead(own)
    m2 = ahead(s0)
    f = aside(m1)
    s1 = sibling(m1)
    s2 = sibling(m2)
    s3 = sibling(f)
    return [own, s0, m1, m2, s2, s1, f, s3]


PHASES = ((24, (8, 8)), (16, (10, 6)))
PARTS = 16
CALLS = ((1, 2), (2, 1))
TURNED = (True, True)


def local_phased(cholesky, green_half, partners):
    return phased(cholesky, green_half, partners)


def phased(cholesky, green_half, partners):
    blocks, orbs = lax.axis_size("loop"), lax.axis_size("orb")
    rows, width = green_half.shape
    per_block = partners.shape[0] // blocks
    tile = 1024
    events = partners.T
    spans, phases, low = [], [], 0
    for size, cuts in PHASES:
        left = 0
        for cut in cuts:
            spans.append((low, low + size, left, left + cut * (width // PARTS)))
            left = spans[-1][3]
        phases.append((low, low + size))
        low += size
    own = [None] * len(spans)
    for half in range(2):
        chosen = [i for i, span in enumerate(spans) if (span[2] > 0) == half]
        outs = select_rows(events, green_half, per_block, [spans[i] for i in chosen], 2048)
        for i, out in zip(chosen, outs):
            own[i] = out
    cholesky = load(cholesky)
    sends, orders, pick = make_tables(events, rows, blocks, orbs, per_block, tuple(phases))
    groups, first_pieces, at = [], [], 0
    for number, (size, cuts) in enumerate(PHASES):
        total = None
        for c, cut in enumerate(cuts):
            pieces = gather_pieces(own[at], blocks)
            span = spans[at][3] - spans[at][2]
            calls = CALLS[number][c]
            for k in range(calls):
                last = c == len(cuts) - 1 and k == calls - 1
                begin, end = (span // tile * i // calls * tile for i in (k, k + 1))
                table = sends[number] if last else None
                outs = contract(pieces, cholesky, begin, end, spans[at][2], total, table, orbs, tile, TURNED[number])
                total = outs[0]
            if number == 0:
                first_pieces.append(pieces)
            at += 1
        parts = [outs[0]]
        for j in range(orbs - 1, 0, -1):
            parts.append(lax.ppermute(outs[j], "orb", [(i, i ^ j) for i in range(orbs)]))
        groups.append((orders[number], parts))
    new_green = copy_rows(pick, green_half, first_pieces, per_block, 2 * tile)
    base = finish(None, groups[:-1])
    return new_green, finish(base, groups[-1:], 2)


def contract_plain(shard_rows, cholesky):
    return lax.dot_general(shard_rows, cholesky, CONTRACT_LAST, preferred_element_type=F32)


def local_gathered(cholesky, green_half, partners):
    loop_count = lax.axis_size("loop")
    block_rows = green_half.shape[0]
    walkers = block_rows * loop_count
    per_block = partners.shape[0] // loop_count
    sources, targets = partners[:, 0], partners[:, 1]
    first_row = lax.axis_index("loop") * block_rows
    walker_index = jnp.arange(walkers, dtype=I32)
    hits = targets[None, :] == walker_index[:, None]
    overwritten = jnp.any(hits, axis=1)
    anchor = jnp.where(overwritten, jnp.sum(jnp.where(hits, sources[None, :], 0), axis=1), walker_index)
    local_flags = lax.dynamic_slice_in_dim(overwritten, first_row, block_rows)
    local_targets = jnp.nonzero(local_flags, size=per_block)[0].astype(I32)
    local_anchor = jnp.take(anchor, first_row + local_targets)
    shard_rows = lax.all_gather(green_half, "loop", axis=0, tiled=True)
    bias = contract_plain(shard_rows, cholesky)
    select = (local_anchor[:, None] == walker_index[None, :]).astype(BF16)
    copied = dot(select, shard_rows).astype(BF16)
    new_green = green_half.at[local_targets].set(copied)
    full_bias = jnp.take(bias, anchor, axis=0)
    return new_green, lax.psum_scatter(full_bias, "orb", scatter_dimension=0, tiled=True)


def solution(mesh):
    blocks, orbs = mesh.shape["loop"], mesh.shape["orb"]
    cube = blocks == 2**3 and orbs == 2**2
    return jax.shard_map(
        local_phased if cube else local_gathered,
        mesh=mesh,
        in_specs=(P("loop", "orb"), P("loop", "orb"), P()),
        out_specs=(P("loop", "orb"), P("orb", "loop")),
        check_vma=False,
    )
```
